256 devices in a mesh: clip: 4 (over z_lo), frame: 16 (over x, y), mp: 4 (over z_hi, core).
Axes of the slice: x: 4, y: 4, z: 8 (z_hi: 2, z_lo: 4; z = z_hi * 4 + z_lo), core: 2. Of those that a mesh axis runs over, the one named last changes fastest.
Arguments:
- query_spatial: bfloat16 [4, 16, 16, 40, 2560], P('clip', 'frame', None, None, 'mp'), may hold values from -24 to 24
- key_spatial: bfloat16 [4, 16, 16, 40, 2560], P('clip', 'frame', None, None, 'mp'), may hold values from -24 to 24
- value_spatial: bfloat16 [4, 16, 16, 40, 2560], P('clip', 'frame', None, None, 'mp'), may hold values from -10 to 10
- gains: float32 [3, 2560], P(None, 'mp'), may hold values from 0.5 to 2.5
- warp_lists: int32 [4, 16, 16], P('clip', 'frame'), may hold values from 0 to 15
- cotangent: bfloat16 [4, 16, 16, 40, 2560], P('clip', None, 'frame', None, 'mp'), may hold values from -3 to 3
Outputs:
- temporal_out: bfloat16 [4, 16, 16, 40, 2560], P('clip', None, 'frame', None, 'mp')
- grad_query: bfloat16 [4, 16, 16, 40, 2560], P('clip', 'frame', None, None, 'mp')
- grad_key: bfloat16 [4, 16, 16, 40, 2560], P('clip', 'frame', None, None, 'mp')
- grad_value: bfloat16 [4, 16, 16, 40, 2560], P('clip', 'frame', None, None, 'mp')
- grad_gains: float32 [3, 2560], P(None, 'mp')
The draws below stay inside these ranges and needn't reach their ends.
All inputs are finite; a program needn't handle non-finite values.
Results may differ from the reference program's by a relative error of at most 0.035.
Values may be sent and summed in bfloat16 or wider, within the bound.
No kernel may reach another device: no remote copies, remote signals or barrier semaphores. Data moves between devices by JAX's collectives and lax.ppermute only.
A program may use at most 128 MiB of HBM per device.

```python
import math
import jax
import jax.numpy as jnp
from jax import lax

HEADS = 20
HD = 128
TT = 40
WIDTH = 2560
CLIPS = 4
FRAMES = 16
TILES = 16


def pair_draw(key):
    key_first, key_second = jax.random.split(jax.random.fold_in(key, 17), 2)
    shape = (CLIPS, FRAMES, TILES, TT, HEADS * HD)
    query_all = 1.6 * jax.random.normal(key_first, shape, jnp.float32)
    key_all = 1.6 * jax.random.normal(key_second, shape, jnp.float32)
    return (jnp.clip(query_all, -24.0, 24.0), jnp.clip(key_all, -24.0, 24.0))


def draw_query_spatial(key, part):
    return pair_draw(key)[0].astype(jnp.bfloat16)


def draw_key_spatial(key, part):
    return pair_draw(key)[1].astype(jnp.bfloat16)


def draw_value_spatial(key, part):
    shape = (CLIPS, FRAMES, TILES, TT, HEADS * HD)
    head_of = (jnp.arange(HEADS * HD) // HD).astype(jnp.float32)
    spread = 0.4 * 3.0 ** (head_of / max(HEADS - 1, 1))
    inner_key = jax.random.fold_in(key, 23)
    values = jax.random.normal(inner_key, shape, jnp.float32)
    return jnp.clip(values * spread, -10.0, 10.0).astype(jnp.bfloat16)


def draw_gains(key, part):
    inner_key = jax.random.fold_in(key, 29)
    upper = jnp.log(2.0)
    logs = jax.random.uniform(inner_key, (3, HEADS * HD), jnp.float32, jnp.log(0.5), upper)
    return jnp.exp(logs)


def with_ends(entries, key, low, largest):
    longest = entries.shape.index(max(entries.shape))
    spots = []
    for shift in (0, 1):
        where = [jax.random.randint(jax.random.fold_in(key, axis), (), 0, length) for axis, length in enumerate(entries.shape)]
        where[longest] = (where[longest] + shift) % entries.shape[longest]
        spots.append(tuple(where))
    return entries.at[spots[0]].set(low).at[spots[1]].set(largest)


def block_scale(key, dims, cuts, least, high):
    gain = 1.0
    for axis_at, blocks in cuts:
        heights = jax.random.uniform(jax.random.fold_in(jax.random.fold_in(key, 6), axis_at), (blocks,), jnp.float32, least / len(cuts), high / len(cuts))
        gain = gain * jnp.repeat(jnp.exp(heights), dims[axis_at] // blocks).reshape((-1,) + (1,) * (len(dims) - 1 - axis_at))
    return gain


def gaussian(key, dims, deviation, reach, cuts=(), kind=jnp.bfloat16):
    level = block_scale(key, dims, cuts, -0.22, 0.18) if cuts else 1.0
    values = jax.random.normal(key, dims, jnp.float32) * deviation * level
    return jnp.minimum(jnp.maximum(values, -reach), reach).astype(kind)


def setup_inputs(seed: int = 0) -> dict:
    keys = jax.random.split(jax.random.key(seed), 7)
    query_spatial = draw_query_spatial(jax.random.fold_in(keys[6], 71), 0)
    key_spatial = draw_key_spatial(jax.random.fold_in(keys[6], 71), 0)
    value_spatial = draw_value_spatial(jax.random.fold_in(keys[6], 71), 0)
    gains = draw_gains(jax.random.fold_in(keys[6], 71), 0)
    warp_lists = with_ends(jax.random.randint(keys[4], (CLIPS, FRAMES, TILES), 0, TILES), jax.random.fold_in(keys[4], 1), 0, TILES - 1).astype(jnp.int32)
    cotangent = gaussian(keys[5], (CLIPS, FRAMES, TILES, TT, WIDTH), 0.5, 3.0, ((0, 4), (2, 16), (4, 4)))
    return dict(query_spatial=query_spatial, key_spatial=key_spatial, value_spatial=value_spatial, gains=gains, warp_lists=warp_lists, cotangent=cotangent)


epsilon = 1e-06

def attend_weights(queries, key_rows, visible):
    head_dim = queries.shape[-1]
    scores = jnp.einsum('qhd,khd->hqk', queries.astype(jnp.float32), key_rows.astype(jnp.float32)) / math.sqrt(head_dim)
    scores = jnp.where(visible[None], scores, -1e+30)
    top = lax.optimization_barrier(jnp.max(scores, axis=-1, keepdims=True))
    expon = jnp.exp(scores - top)
    return expon / lax.optimization_barrier(jnp.sum(expon, axis=-1, keepdims=True))

def attend_forward(queries, key_rows, value_rows, visible):
    weights = attend_weights(queries, key_rows, visible)
    rounded = weights.astype(jnp.bfloat16)
    output = jnp.einsum('hqk,khd->qhd', rounded.astype(jnp.float32), value_rows.astype(jnp.float32))
    return output.astype(jnp.bfloat16)

def attend_backward(queries, key_rows, value_rows, upstream, visible):
    head_dim = queries.shape[-1]
    weights = attend_weights(queries, key_rows, visible)
    rounded = weights.astype(jnp.bfloat16)
    grad_weights = jnp.einsum('qhd,khd->hqk', upstream.astype(jnp.float32), value_rows.astype(jnp.float32))
    inner = lax.optimization_barrier(jnp.sum(weights * grad_weights, axis=-1, keepdims=True))
    grad_scores = (weights * (grad_weights - inner) / math.sqrt(head_dim)).astype(jnp.bfloat16)
    grad_queries = jnp.einsum('hqk,khd->qhd', grad_scores.astype(jnp.float32), key_rows.astype(jnp.float32))
    grad_keys = jnp.einsum('hqk,qhd->khd', grad_scores.astype(jnp.float32), queries.astype(jnp.float32))
    grad_values = jnp.einsum('hqk,qhd->khd', rounded.astype(jnp.float32), upstream.astype(jnp.float32))
    return (grad_queries, grad_keys, grad_values)

def reference(query_spatial, key_spatial, value_spatial, gains, warp_lists, cotangent):
    gain_query = gains[0]
    gain_key = gains[1]
    gain_value = gains[2]

    def one_clip(inputs):
        query_clip, key_clip, value_clip, warp_clip, cotan_clip = inputs
        frames, tiles, tile_tok, width = query_clip.shape
        heads = width // HD
        count = tiles * tile_tok

        def to_heads(array):
            return array.reshape(frames, count, heads, HD)
        all_visible = jnp.ones((count, count), bool)
        spatial = lax.map(lambda trio: attend_forward(trio[0], trio[1], trio[2], all_visible), (to_heads(query_clip), to_heads(key_clip), to_heads(value_clip)))
        spatial = spatial.reshape(frames, tiles, tile_tok, width)
        spatial_f = spatial.astype(jnp.float32)
        inverse = lax.rsqrt(lax.optimization_barrier(jnp.mean(spatial_f * spatial_f, axis=-1, keepdims=True)) + epsilon)
        normed = (spatial_f * inverse).astype(jnp.bfloat16)
        warped = jax.vmap(lambda field, rows: field[rows])(normed, warp_clip)
        tile_query = (normed.astype(jnp.float32) * gain_query).astype(jnp.bfloat16)
        tile_key = (warped.astype(jnp.float32) * gain_key).astype(jnp.bfloat16)
        tile_value = (warped.astype(jnp.float32) * gain_value).astype(jnp.bfloat16)

        def tile_major(array):
            return jnp.transpose(array, (1, 0, 2, 3)).reshape(tiles, frames * tile_tok, heads, HD)

        def frame_major(array):
            return jnp.transpose(array.reshape(tiles, frames, tile_tok, width), (1, 0, 2, 3))
        frame_of = jnp.arange(frames * tile_tok) // tile_tok
        causal = frame_of[:, None] >= frame_of[None, :]
        temporal = lax.map(lambda trio: attend_forward(trio[0], trio[1], trio[2], causal), (tile_major(tile_query), tile_major(tile_key), tile_major(tile_value)))
        grads = lax.map(lambda quad: attend_backward(quad[0], quad[1], quad[2], quad[3], causal), (tile_major(tile_query), tile_major(tile_key), tile_major(tile_value), tile_major(cotan_clip)))
        rounded = lax.optimization_barrier((grads[0].astype(jnp.bfloat16), grads[1].astype(jnp.bfloat16), grads[2].astype(jnp.bfloat16)))
        grad_tq = frame_major(rounded[0]).astype(jnp.float32)
        grad_tk = frame_major(rounded[1]).astype(jnp.float32)
        grad_tv = frame_major(rounded[2]).astype(jnp.float32)
        gain_terms = jnp.stack([lax.optimization_barrier(jnp.sum(grad_tq * normed.astype(jnp.float32), axis=(0, 1, 2))), lax.optimization_barrier(jnp.sum(grad_tk * warped.astype(jnp.float32), axis=(0, 1, 2))), lax.optimization_barrier(jnp.sum(grad_tv * warped.astype(jnp.float32), axis=(0, 1, 2)))])
        direct = grad_tq * gain_query
        moved = grad_tk * gain_key + grad_tv * gain_value
        onehot = (warp_clip[:, :, None] == jnp.arange(tiles)[None, None, :]).astype(jnp.float32)
        grad_normed = direct + jnp.einsum('tjs,tjaf->tsaf', onehot, moved, precision=lax.Precision.HIGHEST)
        inner = lax.optimization_barrier(jnp.mean(grad_normed * spatial_f, axis=-1, keepdims=True))
        grad_spatial = (inverse * grad_normed - spatial_f * inverse ** 3 * inner).astype(jnp.bfloat16)
        back = lax.map(lambda quad: attend_backward(quad[0], quad[1], quad[2], quad[3], all_visible), (to_heads(query_clip), to_heads(key_clip), to_heads(value_clip), to_heads(grad_spatial)))
        shape = (frames, tiles, tile_tok, width)
        return (frame_major(temporal), back[0].reshape(shape).astype(jnp.bfloat16), back[1].reshape(shape).astype(jnp.bfloat16), back[2].reshape(shape).astype(jnp.bfloat16), gain_terms)
    results = lax.map(one_clip, (query_spatial, key_spatial, value_spatial, warp_lists, cotangent))
    return (results[0], results[1], results[2], results[3], lax.optimization_barrier(jnp.sum(results[4], axis=0)))
```

```python
import functools
import math

import jax
import jax.numpy as jnp
from jax import lax
from jax.experimental import pallas as pl
from jax.experimental.pallas import tpu as pltpu
from jax.sharding import PartitionSpec as P

HEADS = 20
HD = 128
TILES = 16
TT = 40
TOK = TILES * TT
WIDTH = HEADS * HD
EPS = 1e-06
SCALE = 1.0 / math.sqrt(HD)
LOG2E = math.log2(math.e)
RB = 128
F32 = jnp.float32
BF16 = jnp.bfloat16


def dot_nt(a, b):
    return lax.dot_general(a, b, (((1,), (1,)), ((), ())), preferred_element_type=F32)


def dot_nn(a, b):
    return lax.dot_general(a, b, (((1,), (0,)), ((), ())), preferred_element_type=F32)


def row_sums(x):
    ones = jnp.ones((8, x.shape[1]), F32)
    return lax.dot_general(
        ones, x, (((1,), (1,)), ((), ())), preferred_element_type=F32, precision=lax.Precision.HIGHEST
    )


def as_column(row):
    tall = jnp.broadcast_to(row[0:1, :], (128, row.shape[1]))
    return tall.T


def per_block(x, blocks):
    return jnp.concatenate([x] * blocks, axis=1)


def spatial_forward(q_ref, k_ref, v_ref, o_ref, p_ref, ss_ref, vaug):
    vaug[:, :HD] = v_ref[...]
    vaug[:, HD:] = jnp.ones((TOK, HD), BF16)
    k = k_ref[...]
    for i in range(TOK // RB):
        rows = slice(i * RB, (i + 1) * RB)
        s = dot_nt(q_ref[rows, :], k)
        top = jnp.max(s, axis=-1, keepdims=True)
        e = jnp.exp2((s - top) * (SCALE * LOG2E))
        both = dot_nn(e.astype(BF16), vaug[...])
        inv = 1.0 / both[:, HD:]
        p_ref[0, rows, :] = (e * per_block(inv, TOK // HD)).astype(BF16)
        o = (both[:, :HD] * inv).astype(BF16)
        o_ref[rows, :] = o
        of = o.astype(F32)
        part = row_sums(of * of)

        @pl.when(pl.program_id(0) == 0)
        def _():
            ss_ref[:, rows] = part

        @pl.when(pl.program_id(0) > 0)
        def _():
            ss_ref[:, rows] += part


def pack_normed(warp, sp_ref, ss_ref, send_ref, n_ref):
    inv = lax.rsqrt(as_column(ss_ref[...]) / WIDTH + EPS)
    heads = sp_ref.shape[2] // HD
    for j in range(TILES):
        scaled = sp_ref[j].astype(F32) * per_block(inv[j * TT : (j + 1) * TT], heads)
        normed = scaled.astype(BF16)
        n_ref[j] = normed
        send_ref[j, 0] = normed
    for j in range(TILES):
        send_ref[j, 1] = n_ref[warp[j]]


def temporal(rc_ref, g_ref, gain_ref, out_ref, send_ref, terms_ref, qs, ks, vaug, gs, es, ts, ds):
    gq, gk, gv = gain_ref[0:1, :], gain_ref[1:2, :], gain_ref[2:3, :]
    normed = rc_ref[:, 0].astype(F32).reshape(TOK, HD)
    warped = rc_ref[:, 1].astype(F32).reshape(TOK, HD)
    qs[...] = (normed * gq).astype(BF16)
    ks[...] = (warped * gk).astype(BF16)
    vaug[:, :HD] = (warped * gv).astype(BF16)
    vaug[:, HD:] = jnp.ones((TOK, HD), BF16)
    k = ks[...]
    for i in range(TOK // RB):
        rows = slice(i * RB, (i + 1) * RB)
        q = qs[rows, :]
        g = g_ref[rows, :]
        s = dot_nt(q, k)
        row = lax.broadcasted_iota(jnp.int32, (RB, 1), 0) + i * RB
        limit = (lax.div(row, TT) + 1) * TT
        col = lax.broadcasted_iota(jnp.int32, (RB, TOK), 1)
        s = jnp.where(col < limit, s, -1e30)
        top = jnp.max(s, axis=-1, keepdims=True)
        e = jnp.exp2((s - top) * (SCALE * LOG2E))
        eb = e.astype(BF16)
        both = dot_nn(eb, vaug[...])
        inv = 1.0 / both[:, HD:]
        o = both[:, :HD] * inv
        out_ref[rows, :] = o.astype(BF16)
        gf = g.astype(F32)
        inner = jnp.sum(gf * o, axis=-1, keepdims=True)
        dp = dot_nt(g, vaug[:, :HD])
        t = (e * (dp - inner)).astype(BF16)
        es[rows, :] = eb
        ts[rows, :] = t
        ds[rows, :] = (dot_nn(t, k) * (inv * SCALE)).astype(BF16)
        gs[rows, :] = gf * inv
        qs[rows, :] = (q.astype(F32) * (inv * SCALE)).astype(BF16)
    dk = dot_nn(qs[...].T, ts[...]).T.astype(BF16).astype(F32)
    dv = dot_nn(gs[...].T.astype(BF16), es[...]).T.astype(BF16).astype(F32)
    dq = ds[...].astype(F32)
    send_ref[:, 0] = (dq * gq).reshape(TILES, TT, HD).astype(BF16)
    send_ref[:, 1] = (dk * gk + dv * gv).reshape(TILES, TT, HD).astype(BF16)
    terms_ref[0:1, :] = jnp.sum(dq * normed, axis=0, keepdims=True)
    terms_ref[1:2, :] = jnp.sum(dk * warped, axis=0, keepdims=True)
    terms_ref[2:3, :] = jnp.sum(dv * warped, axis=0, keepdims=True)


def gather_back(warp, rc_ref, sp_ref, gn_ref, in_ref):
    for j in range(TILES):
        gn_ref[j] = rc_ref[j, 0].astype(F32)
    for j in range(TILES):
        gn_ref[warp[j]] += rc_ref[j, 1].astype(F32)
    prod = gn_ref[...] * sp_ref[...].astype(F32)
    in_ref[...] = row_sums(prod.reshape(TOK, sp_ref.shape[2]))


def spatial_backward(
    q_ref, k_ref, v_ref, p_ref, sp_ref, gn_ref, ss_ref, in_ref, dq_ref, dk_ref, dv_ref, gb, ts
):
    inv = lax.rsqrt(as_column(ss_ref[...]) / WIDTH + EPS)
    shift = inv * inv * inv * (as_column(in_ref[...]) / WIDTH)
    spatial = sp_ref[...].astype(F32)
    grad = inv * gn_ref[...] - spatial * shift
    gb[...] = grad
    for i in range(TOK // RB):
        rows = slice(i * RB, (i + 1) * RB)
        g = gb[rows, :].astype(BF16)
        inner = jnp.sum(g.astype(F32) * sp_ref[rows, :].astype(F32), axis=-1, keepdims=True)
        dp = dot_nt(g, v_ref[...])
        t = (p_ref[0, rows, :].astype(F32) * (dp - inner)).astype(BF16)
        ts[rows, :] = t
        dq_ref[rows, :] = (dot_nn(t, k_ref[...]) * SCALE).astype(BF16)
    dk_ref[...] = (dot_nn(q_ref[...].T, ts[...]).T * SCALE).astype(BF16)
    dv_ref[...] = dot_nn(gb[...].T.astype(BF16), p_ref[0]).T.astype(BF16)


def whole(shape):
    return pl.BlockSpec(shape, lambda *_: (0,) * len(shape))


def head_columns():
    return pl.BlockSpec((TOK, HD), lambda h, *_: (0, h))


def params():
    return pltpu.CompilerParams(vmem_limit_bytes=50 * 1024 * 1024)


def summed_over_mp(x):
    x = x + lax.ppermute(x, "mp", [(i, i ^ 1) for i in range(4)])
    return x + lax.ppermute(x, "mp", [(i, i ^ 2) for i in range(4)])


def body(query_spatial, key_spatial, value_spatial, gains, warp_lists, cotangent):
    width = query_spatial.shape[4]
    heads = width // HD
    frame_shape = query_spatial.shape
    tile_shape = cotangent.shape
    q = query_spatial.reshape(TOK, width)
    k = key_spatial.reshape(TOK, width)
    v = value_spatial.reshape(TOK, width)
    g = cotangent.reshape(TOK, width)
    warp = warp_lists[0, 0]
    sds = jax.ShapeDtypeStruct

    spatial, probs, squares = pl.pallas_call(
        spatial_forward,
        grid=(heads,),
        in_specs=[head_columns()] * 3,
        out_specs=[
            head_columns(),
            pl.BlockSpec((1, TOK, TOK), lambda h: (h, 0, 0)),
            whole((8, TOK)),
        ],
        out_shape=[sds((TOK, width), BF16), sds((heads, TOK, TOK), BF16), sds((8, TOK), F32)],
        scratch_shapes=[pltpu.VMEM((TOK, 2 * HD), BF16)],
        compiler_params=params(),
        name="spatial_forward",
    )(q, k, v)
    squares = summed_over_mp(squares)
    spatial3 = spatial.reshape(TILES, TT, width)

    send = pl.pallas_call(
        pack_normed,
        grid_spec=pltpu.PrefetchScalarGridSpec(
            num_scalar_prefetch=1,
            grid=(1,),
            in_specs=[whole((TILES, TT, width)), whole((8, TOK))],
            out_specs=whole((TILES, 2, TT, width)),
            scratch_shapes=[pltpu.VMEM((TILES, TT, width), BF16)],
        ),
        out_shape=sds((TILES, 2, TT, width), BF16),
        compiler_params=params(),
        name="pack_normed",
    )(warp, spatial3, squares)
    got = lax.all_to_all(send, "frame", 0, 0, tiled=True)

    per_head = pl.BlockSpec((TILES, 2, TT, HD), lambda h: (0, 0, 0, h))
    big = pltpu.VMEM((TOK, TOK), BF16)
    out, back, terms = pl.pallas_call(
        temporal,
        grid=(heads,),
        in_specs=[per_head, head_columns(), pl.BlockSpec((3, HD), lambda h: (0, h))],
        out_specs=[head_columns(), per_head, pl.BlockSpec((3, HD), lambda h: (0, h))],
        out_shape=[
            sds((TOK, width), BF16),
            sds((TILES, 2, TT, width), BF16),
            sds((3, width), F32),
        ],
        scratch_shapes=[
            pltpu.VMEM((TOK, HD), BF16),
            pltpu.VMEM((TOK, HD), BF16),
            pltpu.VMEM((TOK, 2 * HD), BF16),
            pltpu.VMEM((TOK, HD), F32),
            big,
            big,
            pltpu.VMEM((TOK, HD), BF16),
        ],
        compiler_params=params(),
        name="temporal",
    )(got, g, gains)
    came = lax.all_to_all(back, "frame", 0, 0, tiled=True)
    everyone = jnp.broadcast_to(terms[None], (64, *terms.shape))
    grad_gains = lax.all_to_all(everyone, ("clip", "frame"), 0, 0, tiled=True).sum(axis=0)

    grad_normed, inner = pl.pallas_call(
        gather_back,
        grid_spec=pltpu.PrefetchScalarGridSpec(
            num_scalar_prefetch=1,
            grid=(1,),
            in_specs=[whole((TILES, 2, TT, width)), whole((TILES, TT, width))],
            out_specs=[whole((TILES, TT, width)), whole((8, TOK))],
        ),
        out_shape=[sds((TILES, TT, width), F32), sds((8, TOK), F32)],
        compiler_params=params(),
        name="gather_back",
    )(warp, came, spatial3)
    inner = summed_over_mp(inner)

    dq, dk, dv = pl.pallas_call(
        spatial_backward,
        grid=(heads,),
        in_specs=[head_columns()] * 3
        + [pl.BlockSpec((1, TOK, TOK), lambda h: (h, 0, 0))]
        + [head_columns()] * 2
        + [whole((8, TOK))] * 2,
        out_specs=[head_columns()] * 3,
        out_shape=[sds((TOK, width), BF16)] * 3,
        scratch_shapes=[pltpu.VMEM((TOK, HD), F32), big],
        compiler_params=params(),
        name="spatial_backward",
    )(q, k, v, probs, spatial, grad_normed.reshape(TOK, width), squares, inner)
    return (
        out.reshape(tile_shape),
        dq.reshape(frame_shape),
        dk.reshape(frame_shape),
        dv.reshape(frame_shape),
        grad_gains,
    )


def solution(mesh):
    frames = P("clip", "frame", None, None, "mp")
    tiles = P("clip", None, "frame", None, "mp")
    return jax.shard_map(
        body,
        mesh=mesh,
        in_specs=(frames, frames, frames, P(None, "mp"), P("clip", "frame", None), tiles),
        out_specs=(tiles, frames, frames, frames, P(None, "mp")),
        check_vma=False,
    )
```

```python
import math

import jax
import jax.numpy as jnp
from jax import lax
from jax.experimental import pallas as pl
from jax.experimental.pallas import tpu as pltpu
from jax.sharding import PartitionSpec as P


HEADS = 20
HD = 128
TILES = 16
TT = 40
TOK = TILES * TT
WIDTH = HEADS * HD
HERE = 5
EPS = 1e-06
SCALE = 1.0 / math.sqrt(HD)
LOG2E = math.log2(math.e)
RB = 128
BLOCKS = TOK // RB
F32 = jnp.float32
BF16 = jnp.bfloat16


def dot_nt(a, b):
    return lax.dot_general(a, b, (((1,), (1,)), ((), ())), preferred_element_type=F32)


def dot_nn(a, b):
    return lax.dot_general(a, b, (((1,), (0,)), ((), ())), preferred_element_type=F32)


def row_sums(x):
    ones = jnp.ones((8, x.shape[1]), F32)
    return lax.dot_general(
        ones, x, (((1,), (1,)), ((), ())), preferred_element_type=F32, precision=lax.Precision.HIGHEST
    )


def column_sum(x):
    x = jnp.sum(x.reshape(10, 64, HD), axis=0)
    return jnp.sum(x, axis=0, keepdims=True)


def as_column(row):
    return jnp.broadcast_to(row, (128, row.shape[1])).T


def softmax_rows(s):
    top = jnp.max(s, axis=-1, keepdims=True)
    e = jnp.exp2((s - top) * (SCALE * LOG2E))
    return (e * (1.0 / jnp.sum(e, axis=-1, keepdims=True))).astype(BF16)


def across(x_t):
    x_t = x_t.astype(BF16)
    r = lax.broadcasted_iota(jnp.int32, (HD, HD), 0)
    c = lax.broadcasted_iota(jnp.int32, (HD, HD), 1)
    eye = jnp.where(r == c, 1.0, 0.0).astype(BF16)
    parts = [dot_nt(eye, x_t[:, i : i + HD]) for i in range(0, x_t.shape[1], HD)]
    return jnp.concatenate(parts, axis=0)


def spatial_forward(q_ref, k_ref, v_ref, o_ref, p_ref, ss_ref, acc):
    h = pl.program_id(0)

    @pl.when(h == 0)
    def _():
        acc[...] = jnp.zeros_like(acc)

    k = k_ref[...]
    v = v_ref[...]
    for i in range(BLOCKS):
        rows = slice(i * RB, (i + 1) * RB)
        p = softmax_rows(dot_nt(q_ref[rows, :], k))
        p_ref[0, rows, :] = p
        o = dot_nn(p, v).astype(BF16)
        o_ref[rows, :] = o
        of = o.astype(F32)
        acc[rows, :] += of * of

    @pl.when(h == pl.num_programs(0) - 1)
    def _():
        ss_ref[...] = row_sums(acc[...])[0:1]


def pack_normed(warp, sp_ref, one_ref, two_ref, send_ref, inv_ref, n_ref):
    @pl.when(pl.program_id(0) == 0)
    def _():
        inv = lax.rsqrt((one_ref[...] + two_ref[...]) / WIDTH + EPS)
        inv_ref[...] = as_column(inv).reshape(TILES, TT, HD)

    normed = (sp_ref[...].astype(F32) * inv_ref[...]).astype(BF16)
    n_ref[...] = normed
    send_ref[:, 0] = normed
    for j in range(TILES):
        send_ref[j, 1] = n_ref[warp[j]]


def temporal(
    rc_ref, g_ref, gain_ref, out_ref, send_ref, terms_ref, qs, ks, vs, ps, ts, ds
):
    h = pl.program_id(0)

    @pl.when(h == 0)
    def _():
        ps[...] = jnp.zeros_like(ps)
        ts[...] = jnp.zeros_like(ts)

    gq, gk, gv = gain_ref[0:1, :], gain_ref[1:2, :], gain_ref[2:3, :]
    normed = rc_ref[:, 0].astype(F32).reshape(TOK, HD)
    warped = rc_ref[:, 1].astype(F32).reshape(TOK, HD)
    qs[...] = (normed * gq).astype(BF16)
    ks[...] = (warped * gk).astype(BF16)
    vs[...] = (warped * gv).astype(BF16)
    for i in range(BLOCKS):
        rows = slice(i * RB, (i + 1) * RB)
        last = ((i * RB + RB - 1) // TT + 1) * TT
        keys = max(min(-(-last // HD) * HD, TOK), 2 * HD)
        clear = ((i * RB) // TT + 1) * TT // HD * HD
        g = g_ref[rows, :]
        k = ks[:keys, :]
        v = vs[:keys, :]
        s = dot_nt(qs[rows, :], k)
        row = lax.broadcasted_iota(jnp.int32, (RB, 1), 0).astype(F32) + (i * RB + 0.5)
        limit = (jnp.floor(row * (1.0 / TT)) + 1.0) * TT
        col = lax.broadcasted_iota(jnp.int32, (RB, keys - clear), 1).astype(F32) + clear
        masked = jnp.where(col < limit, s[:, clear:], -1e30)
        s = jnp.concatenate([s[:, :clear], masked], axis=1) if clear else masked
        p = softmax_rows(s)
        ps[rows, :keys] = p
        o = dot_nn(p, v)
        out_ref[rows, :] = o.astype(BF16)
        inner = jnp.sum(g.astype(F32) * o, axis=-1, keepdims=True)
        t = p * (dot_nt(g, v) - inner).astype(BF16)
        ts[rows, :keys] = t
        ds[rows, :] = dot_nn(t, k) * SCALE

    def by_keys(left, right):
        lt = left[...].T
        parts = [
            dot_nn(lt, right[:, : 2 * HD]),
            dot_nn(lt[:, RB:], right[RB:, 2 * HD : 4 * HD]),
            dot_nn(lt[:, 3 * RB :], right[3 * RB :, 4 * HD :]),
        ]
        return jnp.concatenate([across(x) for x in parts], axis=0)

    dk = by_keys(qs, ts) * SCALE
    dv = by_keys(g_ref, ps)
    dq = ds[...]
    normed = rc_ref[:, 0].astype(F32).reshape(TOK, HD)
    warped = rc_ref[:, 1].astype(F32).reshape(TOK, HD)
    send_ref[:, 0] = (dq * gq).reshape(TILES, TT, HD).astype(BF16)
    send_ref[:, 1] = (dk * gk + dv * gv).reshape(TILES, TT, HD).astype(BF16)
    terms_ref[0:1, :] = column_sum(dq * normed)
    terms_ref[1:2, :] = column_sum(dk * warped)
    terms_ref[2:3, :] = column_sum(dv * warped)


def gather_back(warp, rc_ref, sp_ref, gn_ref, in_ref, acc):
    h = pl.program_id(0)
    gn_ref[...] = rc_ref[:, 0].astype(F32)
    for j in range(TILES):
        gn_ref[warp[j]] += rc_ref[j, 1].astype(F32)
    prod = gn_ref[...] * sp_ref[...].astype(F32)

    @pl.when(h == 0)
    def _():
        acc[...] = prod

    @pl.when(h > 0)
    def _():
        acc[...] += prod

    @pl.when(h == pl.num_programs(0) - 1)
    def _():
        in_ref[...] = row_sums(acc[...].reshape(TOK, HD))[0:1]


def spatial_backward(
    q_ref, k_ref, v_ref, p_ref, sp_ref, gn_ref, s1_ref, s2_ref, i1_ref, i2_ref,
    dq_ref, dk_ref, dv_ref, inv_s, shift, gb, ts,
):
    @pl.when(pl.program_id(0) == 0)
    def _():
        inv = lax.rsqrt((s1_ref[...] + s2_ref[...]) / WIDTH + EPS)
        inv_s[...] = as_column(inv)
        shift[...] = as_column(inv * inv * inv * ((i1_ref[...] + i2_ref[...]) / WIDTH))

    k = k_ref[...]
    v = v_ref[...]
    for i in range(BLOCKS):
        rows = slice(i * RB, (i + 1) * RB)
        spatial = sp_ref[rows, :].astype(F32)
        grad = inv_s[rows, :] * gn_ref[rows, :] - spatial * shift[rows, :]
        g = grad.astype(BF16)
        gb[rows, :] = g
        inner = jnp.sum(g.astype(F32) * spatial, axis=-1, keepdims=True)
        t = p_ref[0, rows, :] * (dot_nt(g, v) - inner).astype(BF16)
        ts[rows, :] = t
        dq_ref[rows, :] = (dot_nn(t, k) * SCALE).astype(BF16)
    dk_ref[...] = across(dot_nn(q_ref[...].T, ts[...]) * SCALE).astype(BF16)
    dv_ref[...] = across(dot_nn(gb[...].T, p_ref[0])).astype(BF16)


def whole(shape):
    return pl.BlockSpec(shape, lambda *_: (0,) * len(shape))


def columns(rows=TOK):
    return pl.BlockSpec((rows, HD), lambda h, *_: (0, h))


def call(kernel, in_specs, out_specs, out_shape, scratch, us, prefetch=0, limit=63):
    return pl.pallas_call(
        kernel,
        grid_spec=pltpu.PrefetchScalarGridSpec(
            num_scalar_prefetch=prefetch,
            grid=(HERE,),
            in_specs=in_specs,
            out_specs=out_specs,
            scratch_shapes=scratch,
        ),
        out_shape=out_shape,
        cost_estimate=pl.CostEstimate(
            flops=int(us * 1e6), bytes_accessed=int(us * 3.0e6), transcendentals=0
        ),
        compiler_params=pltpu.CompilerParams(vmem_limit_bytes=limit * 1024 * 1024),
    )


def swapped(x, axis, flip):
    size = lax.axis_size(axis)
    return lax.ppermute(x, axis, [(i, i ^ flip) for i in range(size)])


def half_sums(x, axis):
    x = x + swapped(x, axis, 1)
    return x, swapped(x, axis, 2)


def exchanged(x):
    return lax.all_to_all(x, "frame", 0, 0, tiled=True)


def body(query_spatial, key_spatial, value_spatial, gains, warp_lists, cotangent):
    width = HERE * HD
    q = query_spatial.reshape(TOK, width)
    k = key_spatial.reshape(TOK, width)
    v = value_spatial.reshape(TOK, width)
    g = cotangent.reshape(TOK, width)
    warp = warp_lists[0, 0]
    sds = jax.ShapeDtypeStruct
    tall = pltpu.VMEM((TOK, HD), F32)
    thin = pltpu.VMEM((TOK, HD), BF16)
    big = pltpu.VMEM((TOK, TOK), BF16)
    cube = pltpu.VMEM((TILES, TT, HD), F32)
    square = pl.BlockSpec((1, TOK, TOK), lambda h, *_: (h, 0, 0))
    tiles = pl.BlockSpec((TILES, TT, HD), lambda h, *_: (0, 0, h))
    pairs = pl.BlockSpec((TILES, 2, TT, HD), lambda h, *_: (0, 0, 0, h))
    line = whole((1, TOK))
    both = sds((TILES, 2, TT, width), BF16)
    flat = sds((TOK, width), BF16)

    spatial, probs, squares = call(
        spatial_forward,
        [columns()] * 3,
        [columns(), square, line],
        [flat, sds((HERE, TOK, TOK), BF16), sds((1, TOK), F32)],
        [tall],
        7,
    )(q, k, v)
    ss_one, ss_two = half_sums(squares, "mp")
    spatial_tiles = spatial.reshape(TILES, TT, width)
    send = call(
        pack_normed,
        [tiles, line, line],
        pairs,
        both,
        [cube, pltpu.VMEM((TILES, TT, HD), BF16)],
        1,
        prefetch=1,
    )(warp, spatial_tiles, ss_one, ss_two)
    got = exchanged(send)

    out, back, terms = call(
        temporal,
        [pairs, columns(), columns(3)],
        [columns(), pairs, columns(3)],
        [flat, both, sds((3, width), F32)],
        [thin, thin, thin, big, big, tall],
        16,
    )(got, g, gains)
    came = exchanged(back)
    for axis, flips in (("clip", (1, 2)), ("frame", (1, 2, 4, 8))):
        for flip in flips:
            terms = terms + swapped(terms, axis, flip)

    grad_normed, inner = call(
        gather_back,
        [pairs, tiles],
        [tiles, line],
        [sds((TILES, TT, width), F32), sds((1, TOK), F32)],
        [cube],
        2,
        prefetch=1,
    )(warp, came, spatial_tiles)
    in_one, in_two = half_sums(inner, "mp")

    dq, dk, dv = call(
        spatial_backward,
        [columns()] * 3 + [square] + [columns()] * 2 + [line] * 4,
        [columns()] * 3,
        [flat] * 3,
        [tall, tall, thin, big],
        9,
    )(q, k, v, probs, spatial, grad_normed.reshape(TOK, width), ss_one, ss_two, in_one, in_two)
    return (
        out.reshape(cotangent.shape),
        dq.reshape(query_spatial.shape),
        dk.reshape(query_spatial.shape),
        dv.reshape(query_spatial.shape),
        terms,
    )


def solution(mesh):
    frames = P("clip", "frame", None, None, "mp")
    tiles = P("clip", None, "frame", None, "mp")
    return jax.shard_map(
        body,
        mesh=mesh,
        in_specs=(frames, frames, frames, P(None, "mp"), P("clip", "frame", None), tiles),
        out_specs=(tiles, frames, frames, frames, P(None, "mp")),
        check_vma=False,
    )
```

```python
import math

import jax
import jax.numpy as jnp
from jax import lax
from jax.experimental import pallas as pl
from jax.experimental.pallas import tpu as pltpu
from jax.sharding import PartitionSpec as P


HEADS = 20
HD = 128
TILES = 16
TT = 40
TOK = TILES * TT
WIDTH = HEADS * HD
HERE = 5
EPS = 1e-06
SCALE = 1.0 / math.sqrt(HD)
LOG2E = math.log2(math.e)
RB = 320
BLOCKS = TOK // RB
F32 = jnp.float32
BF16 = jnp.bfloat16


def dot_nt(a, b):
    return lax.dot_general(a, b, (((1,), (1,)), ((), ())), preferred_element_type=F32)


def dot_nn(a, b):
    return lax.dot_general(a, b, (((1,), (0,)), ((), ())), preferred_element_type=F32)


def row_sums(x):
    ones = jnp.ones((8, x.shape[1]), F32)
    return lax.dot_general(
        ones, x, (((1,), (1,)), ((), ())), preferred_element_type=F32, precision=lax.Precision.HIGHEST
    )


def column_sum(x):
    x = jnp.sum(x.reshape(10, 64, HD), axis=0)
    return jnp.sum(x, axis=0, keepdims=True)


def as_column(row):
    return jnp.broadcast_to(row, (128, row.shape[1])).T


def softmax_rows(s):
    top = jnp.max(s, axis=-1, keepdims=True)
    e = jnp.exp2((s - top) * (SCALE * LOG2E))
    return (e * (1.0 / jnp.sum(e, axis=-1, keepdims=True))).astype(BF16)


def lanes(h):
    return pl.ds(pl.multiple_of(h * HD, HD), HD)


def spatial_forward(q_hbm, k_hbm, v_hbm, o_ref, p_ref, ss_ref, q_ref, k_ref, v_ref, acc, sems):
    h = pl.program_id(0)

    @pl.when(h == 0)
    def _():
        copies = [
            pltpu.make_async_copy(a, b, sems.at[i])
            for i, (a, b) in enumerate(((k_hbm, k_ref), (q_hbm, q_ref), (v_hbm, v_ref)))
        ]
        for copy in copies:
            copy.start()
        acc[...] = jnp.zeros_like(acc)
        for copy in copies:
            copy.wait()

    k = k_ref[:, lanes(h)]
    vw = jnp.concatenate([v_ref[:, lanes(h)], jnp.ones((TOK, HD), BF16)], axis=1)
    for i in range(BLOCKS):
        rows = slice(i * RB, (i + 1) * RB)
        p = softmax_rows(dot_nt(q_ref[rows, lanes(h)], k))
        p_ref[h, rows, :] = p
        o = dot_nn(p, vw)[:, :HD].astype(BF16)
        o_ref[rows, lanes(h)] = o
        of = o.astype(F32)
        acc[rows, :] += of * of

    @pl.when(h == HERE - 1)
    def _():
        ss_ref[...] = row_sums(acc[...])[0:1]


def pack_normed(warp, sp_ref, one_ref, two_ref, send_ref, n_ref):
    inv = lax.rsqrt((one_ref[...] + two_ref[...]) / WIDTH + EPS)
    inv = as_column(inv)
    for j in range(TILES):
        col = inv[j * TT : (j + 1) * TT]
        normed = (sp_ref[j].astype(F32) * jnp.concatenate([col] * HERE, axis=1)).astype(BF16)
        n_ref[j] = normed
        send_ref[j, :TT] = normed
    for j in range(TILES):
        send_ref[j, TT:] = n_ref[warp[j]]


def temporal(rc_ref, g_ref, gain_ref, out_ref, send_ref, qs, ks, vs, ps, ts, ds, terms):
    h = pl.program_id(0)

    @pl.when(h == 0)
    def _():
        ps[...] = jnp.zeros_like(ps)
        ts[...] = jnp.zeros_like(ts)

    gq, gk, gv = gain_ref[0:1, lanes(h)], gain_ref[1:2, lanes(h)], gain_ref[2:3, lanes(h)]
    normed = rc_ref[:, :TT, lanes(h)].astype(F32).reshape(TOK, HD)
    warped = rc_ref[:, TT:, lanes(h)].astype(F32).reshape(TOK, HD)
    qs[...] = (normed * gq).astype(BF16)
    ks[...] = (warped * gk).astype(BF16)
    vs[...] = (warped * gv).astype(BF16)
    for i in range(BLOCKS):
        rows = slice(i * RB, (i + 1) * RB)
        last = ((i * RB + RB - 1) // TT + 1) * TT
        keys = max(min(-(-last // HD) * HD, TOK), 2 * HD)
        clear = ((i * RB) // TT + 1) * TT // HD * HD
        g = g_ref[rows, lanes(h)]
        k = ks[:keys, :]
        v = vs[:keys, :]
        s = dot_nt(qs[rows, :], k)
        row = lax.broadcasted_iota(jnp.int32, (RB, 1), 0).astype(F32) + (i * RB + 0.5)
        limit = (jnp.floor(row * (1.0 / TT)) + 1.0) * TT
        col = lax.broadcasted_iota(jnp.int32, (RB, keys - clear), 1).astype(F32) + clear
        masked = jnp.where(col < limit, s[:, clear:], -1e30)
        s = jnp.concatenate([s[:, :clear], masked], axis=1) if clear else masked
        p = softmax_rows(s)
        ps[rows, :keys] = p
        o = dot_nn(p, v)
        out_ref[rows, :] = o.astype(BF16)
        inner = jnp.sum(g.astype(F32) * o, axis=-1, keepdims=True)
        t = p * (dot_nt(g, v) - inner).astype(BF16)
        ts[rows, :keys] = t
        ds[rows, :] = dot_nn(t, k) * SCALE

    def by_keys(lt, right):
        parts = [
            dot_nn(lt, right[:, : 2 * HD]),
            dot_nn(lt[:, HD:], right[HD:, 2 * HD : 4 * HD]),
            dot_nn(lt[:, 3 * HD :], right[3 * HD :, 4 * HD :]),
        ]
        return jnp.concatenate([x.T for x in parts], axis=0)

    dk = by_keys(qs[...].T, ts) * SCALE
    dv = by_keys(g_ref[:, lanes(h)].T, ps)
    dq = ds[...]
    normed = rc_ref[:, :TT, lanes(h)].astype(F32).reshape(TOK, HD)
    warped = rc_ref[:, TT:, lanes(h)].astype(F32).reshape(TOK, HD)
    send_ref[:, :TT, lanes(h)] = (dq * gq).reshape(TILES, TT, HD).astype(BF16)
    send_ref[:, TT : 2 * TT, lanes(h)] = (dk * gk + dv * gv).reshape(TILES, TT, HD).astype(BF16)
    terms[0:1, :] = column_sum(dq * normed)
    terms[1:2, :] = column_sum(dk * warped)
    terms[2:3, :] = column_sum(dv * warped)
    high = terms[0:3].astype(BF16).astype(F32)
    low = terms[0:3] - high
    send_ref[:, 2 * TT :, lanes(h)] = jnp.broadcast_to(
        jnp.concatenate([high, low, high[0:2]], axis=0)[None], (TILES, 8, HD)
    ).astype(BF16)


def gather_back(warp, rc_ref, sp_ref, gn_ref, in_ref, terms_ref):
    gn_ref[...] = rc_ref[:, :TT].astype(F32)
    for j in range(TILES):
        gn_ref[warp[j]] += rc_ref[j, TT : 2 * TT].astype(F32)
    total = jnp.sum(rc_ref[:, 2 * TT :].astype(F32), axis=0)
    terms_ref[...] = total[0:3] + total[3:6]
    prod = gn_ref[...] * sp_ref[...].astype(F32)
    prod = prod.reshape(TOK, HERE * HD)
    prod = sum(prod[:, h * HD : (h + 1) * HD] for h in range(HERE))
    in_ref[...] = row_sums(prod)[0:1]


def spatial_backward(
    q_ref, k_ref, v_ref, p_ref, sp_ref, gn_ref, s1_ref, s2_ref, i1_ref, i2_ref,
    dq_ref, dk_ref, dv_ref, inv_s, shift, gb, ts,
):
    h = pl.program_id(0)

    @pl.when(h == 0)
    def _():
        inv = lax.rsqrt((s1_ref[...] + s2_ref[...]) / WIDTH + EPS)
        inv_s[...] = as_column(inv)
        shift[...] = as_column(inv * inv * inv * ((i1_ref[...] + i2_ref[...]) / WIDTH))

    k = k_ref[:, lanes(h)]
    v = v_ref[:, lanes(h)]
    for i in range(BLOCKS):
        rows = slice(i * RB, (i + 1) * RB)
        spatial = sp_ref[rows, lanes(h)].astype(F32)
        grad = inv_s[rows, :] * gn_ref[rows, lanes(h)] - spatial * shift[rows, :]
        g = grad.astype(BF16)
        gb[rows, :] = g
        inner = jnp.sum(g.astype(F32) * spatial, axis=-1, keepdims=True)
        t = p_ref[h, rows, :] * (dot_nt(g, v) - inner).astype(BF16)
        ts[rows, :] = t
        dq_ref[rows, :] = (dot_nn(t, k) * SCALE).astype(BF16)
    dk_ref[...] = (dot_nn(q_ref[:, lanes(h)].T, ts[...]) * SCALE).T.astype(BF16)
    dv_ref[...] = dot_nn(gb[...].T, p_ref[h]).T.astype(BF16)


def columns(rows=TOK):
    return pl.BlockSpec((rows, HD), lambda h, *_: (0, h))


def call(kernel, grid, in_specs, out_specs, out_shape, scratch, us, prefetch=0, limit=24):
    return pl.pallas_call(
        kernel,
        grid_spec=pltpu.PrefetchScalarGridSpec(
            num_scalar_prefetch=prefetch,
            grid=grid,
            in_specs=in_specs,
            out_specs=out_specs,
            scratch_shapes=scratch,
        ),
        out_shape=out_shape,
        cost_estimate=pl.CostEstimate(
            flops=int(us * 1e6), bytes_accessed=int(us * 3.0e6), transcendentals=0
        ),
        compiler_params=pltpu.CompilerParams(vmem_limit_bytes=limit * 1024 * 1024),
    )


def swapped(x, axis, flip):
    size = lax.axis_size(axis)
    return lax.ppermute(x, axis, [(i, i ^ flip) for i in range(size)])


def half_sums(x, axis):
    other = swapped(x, axis, 1)
    x = x + other
    return x, swapped(x, axis, 2)


def exchanged(x):
    return lax.all_to_all(x, "frame", 0, 0, tiled=True)


def body(query_spatial, key_spatial, value_spatial, gains, warp_lists, cotangent):
    width = HERE * HD
    q = query_spatial.reshape(TOK, width)
    k = key_spatial.reshape(TOK, width)
    v = value_spatial.reshape(TOK, width)
    g = cotangent.reshape(TOK, width)
    warp = warp_lists[0, 0]
    sds = jax.ShapeDtypeStruct
    tall = pltpu.VMEM((TOK, HD), F32)
    thin = pltpu.VMEM((TOK, HD), BF16)
    big = pltpu.VMEM((TOK, TOK), BF16)
    held = pl.BlockSpec(memory_space=pltpu.VMEM)
    away = pl.BlockSpec(memory_space=pltpu.HBM)
    line = sds((1, TOK), F32)
    flat = sds((TOK, width), BF16)
    three = sds((3, width), F32)
    heads = (HERE,)

    spatial, probs, squares = call(
        spatial_forward,
        heads,
        [away] * 3,
        [held] * 3,
        [flat, sds((HERE, TOK, TOK), BF16), line],
        [big, big, big, tall, pltpu.SemaphoreType.DMA((3,))],
        7,
    )(*(pltpu.with_memory_space_constraint(x, pltpu.HBM) for x in (q, k, v)))
    ss_one, ss_two = half_sums(squares, "mp")
    spatial_tiles = spatial.reshape(TILES, TT, width)
    send = call(
        pack_normed,
        (),
        [held] * 3,
        held,
        sds((TILES, 2 * TT, width), BF16),
        [pltpu.VMEM((TILES, TT, width), BF16)],
        1,
        prefetch=1,
    )(warp, spatial_tiles, ss_one, ss_two)
    got = exchanged(send)

    out, back = call(
        temporal,
        heads,
        [held] * 3,
        [columns(), held],
        [flat, sds((TILES, 2 * TT + 8, width), BF16)],
        [thin, thin, thin, big, big, tall, pltpu.VMEM((8, HD), F32)],
        16,
    )(got, g, gains)
    came = exchanged(back)

    grad_normed, inner, terms = call(
        gather_back,
        (),
        [held] * 2,
        [held] * 3,
        [sds((TILES, TT, width), F32), line, three],
        [],
        2,
        prefetch=1,
    )(warp, came, spatial_tiles)
    in_one, in_two = half_sums(inner, "mp")
    t_one, t_two = half_sums(terms, "clip")

    dq, dk, dv = call(
        spatial_backward,
        heads,
        [held] * 10,
        [columns()] * 3,
        [flat] * 3,
        [tall, tall, thin, big],
        9,
    )(
        q, k, v, probs, spatial, grad_normed.reshape(TOK, width),
        ss_one, ss_two, in_one, in_two,
    )
    return (
        out.reshape(cotangent.shape),
        dq.reshape(query_spatial.shape),
        dk.reshape(query_spatial.shape),
        dv.reshape(query_spatial.shape),
        t_one + t_two,
    )


def solution(mesh):
    frames = P("clip", "frame", None, None, "mp")
    tiles = P("clip", None, "frame", None, "mp")
    return jax.shard_map(
        body,
        mesh=mesh,
        in_specs=(frames, frames, frames, P(None, "mp"), P("clip", "frame", None), tiles),
        out_specs=(tiles, frames, frames, frames, P(None, "mp")),
        check_vma=False,
    )
```

```python
import math

import jax
import jax.numpy as jnp
from jax import lax
from jax.experimental import pallas as pl
from jax.experimental.pallas import tpu as pltpu
from jax.sharding import PartitionSpec as P


HEADS = 20
HD = 128
TILES = 16
TT = 40
TOK = TILES * TT
WIDTH = HEADS * HD
HERE = 5
EPS = 1e-06
SCALE = 1.0 / math.sqrt(HD)
LOG2E = math.log2(math.e)
RB = 320
SUB = 160
BLOCKS = TOK // RB
F32 = jnp.float32
BF16 = jnp.bfloat16


def dot_nt(a, b):
    return lax.dot_general(a, b, (((1,), (1,)), ((), ())), preferred_element_type=F32)


def dot_nn(a, b):
    return lax.dot_general(a, b, (((1,), (0,)), ((), ())), preferred_element_type=F32)


def row_sums(x):
    ones = jnp.ones((8, x.shape[1]), F32)
    return lax.dot_general(
        ones, x, (((1,), (1,)), ((), ())), preferred_element_type=F32, precision=lax.Precision.HIGHEST
    )


def column_sum(x):
    x = jnp.sum(x.reshape(10, 64, HD), axis=0)
    return jnp.sum(x, axis=0, keepdims=True)


def as_column(row):
    return jnp.broadcast_to(row, (128, row.shape[1])).T


def softmax_rows(s):
    top = jnp.max(s, axis=-1, keepdims=True)
    e = jnp.exp2((s - top) * (SCALE * LOG2E))
    return (e * (1.0 / jnp.sum(e, axis=-1, keepdims=True))).astype(BF16)


def lanes(h):
    return pl.ds(pl.multiple_of(h * HD, HD), HD)


def spatial_forward(q_hbm, k_hbm, v_hbm, o_ref, p_ref, ss_ref, q_ref, k_ref, v_ref, acc, sems):
    h = pl.program_id(0)

    def copies(n):
        return [
            pltpu.make_async_copy(a.at[:, lanes(n)], b.at[:, lanes(n)], sems.at[i, n])
            for i, (a, b) in enumerate(((k_hbm, k_ref), (q_hbm, q_ref), (v_hbm, v_ref)))
        ]

    @pl.when(h == 0)
    def _():
        for n in range(HERE):
            for copy in copies(n):
                copy.start()
        acc[...] = jnp.zeros_like(acc)

    for copy in copies(h):
        copy.wait()

    k = k_ref[:, lanes(h)]
    vw = jnp.concatenate([v_ref[:, lanes(h)], jnp.ones((TOK, HD), BF16)], axis=1)
    for i in range(BLOCKS):
        rows = slice(i * RB, (i + 1) * RB)
        p = softmax_rows(dot_nt(q_ref[rows, lanes(h)], k))
        p_ref[h, rows, :] = p
        o = dot_nn(p, vw)[:, :HD].astype(BF16)
        o_ref[rows, lanes(h)] = o
        of = o.astype(F32)
        acc[rows, :] += of * of

    @pl.when(h == HERE - 1)
    def _():
        ss_ref[...] = row_sums(acc[...])[0:1]


def pack_normed(warp, sp_ref, one_ref, two_ref, send_ref, n_ref):
    inv = lax.rsqrt((one_ref[...] + two_ref[...]) / WIDTH + EPS)
    inv = as_column(inv)
    for j in range(TILES):
        col = inv[j * TT : (j + 1) * TT]
        normed = (sp_ref[j].astype(F32) * jnp.concatenate([col] * HERE, axis=1)).astype(BF16)
        n_ref[j] = normed
        send_ref[j, :TT] = normed
    for j in range(TILES):
        send_ref[j, TT:] = n_ref[warp[j]]


def temporal(rc_ref, g_ref, gain_ref, out_ref, send_ref, qs, ks, vs, ps, ts, ds, terms):
    h = pl.program_id(0)

    @pl.when(h == 0)
    def _():
        ps[...] = jnp.zeros_like(ps)
        ts[...] = jnp.zeros_like(ts)

    gq, gk, gv = gain_ref[0:1, lanes(h)], gain_ref[1:2, lanes(h)], gain_ref[2:3, lanes(h)]
    normed = rc_ref[:, :TT, lanes(h)].astype(F32).reshape(TOK, HD)
    warped = rc_ref[:, TT:, lanes(h)].astype(F32).reshape(TOK, HD)
    qs[...] = (normed * gq).astype(BF16)
    ks[...] = (warped * gk).astype(BF16)
    vs[...] = (warped * gv).astype(BF16)
    s = dot_nt(qs[...], ks[...])
    spans = []
    for i in range(0, TOK, SUB):
        rows = slice(i, i + SUB)
        last = ((i + SUB - 1) // TT + 1) * TT
        keys = min(-(-last // HD) * HD, TOK)
        clear = (i // TT + 1) * TT // HD * HD
        spans.append((rows, keys))
        row = lax.broadcasted_iota(jnp.int32, (SUB, 1), 0).astype(F32) + (i + 0.5)
        limit = (jnp.floor(row * (1.0 / TT)) + 1.0) * TT
        if clear < keys:
            col = lax.broadcasted_iota(jnp.int32, (SUB, keys - clear), 1).astype(F32) + clear
            part = jnp.where(col < limit, s[rows, clear:keys], -1e30)
            part = jnp.concatenate([s[rows, :clear], part], axis=1) if clear else part
        else:
            part = s[rows, :keys]
        ps[rows, :keys] = softmax_rows(part)
    o = dot_nn(ps[...], vs[...])
    out_ref[...] = o.astype(BF16)
    g = g_ref[:, lanes(h)]
    inner = jnp.sum(g.astype(F32) * o, axis=-1, keepdims=True)
    dp = dot_nt(g, vs[...])
    for rows, keys in spans:
        ts[rows, :keys] = ps[rows, :keys] * (dp[rows, :keys] - inner[rows]).astype(BF16)
    ds[...] = dot_nn(ts[...], ks[...]) * SCALE

    def by_keys(lt, right):
        parts = [
            dot_nn(lt, right[:, : 2 * HD]),
            dot_nn(lt[:, HD:], right[HD:, 2 * HD : 4 * HD]),
            dot_nn(lt[:, 3 * HD :], right[3 * HD :, 4 * HD :]),
        ]
        return jnp.concatenate([x.T for x in parts], axis=0)

    dk = by_keys(qs[...].T, ts) * SCALE
    dv = by_keys(g_ref[:, lanes(h)].T, ps)
    dq = ds[...]
    normed = rc_ref[:, :TT, lanes(h)].astype(F32).reshape(TOK, HD)
    warped = rc_ref[:, TT:, lanes(h)].astype(F32).reshape(TOK, HD)
    send_ref[:, :TT, lanes(h)] = (dq * gq).reshape(TILES, TT, HD).astype(BF16)
    send_ref[:, TT : 2 * TT, lanes(h)] = (dk * gk + dv * gv).reshape(TILES, TT, HD).astype(BF16)
    terms[0:1, :] = column_sum(dq * normed)
    terms[1:2, :] = column_sum(dk * warped)
    terms[2:3, :] = column_sum(dv * warped)
    high = terms[0:3].astype(BF16).astype(F32)
    low = terms[0:3] - high
    send_ref[:, 2 * TT :, lanes(h)] = jnp.broadcast_to(
        jnp.concatenate([high, low, high[0:2]], axis=0)[None], (TILES, 8, HD)
    ).astype(BF16)


def gather_back(warp, rc_ref, sp_ref, gn_ref, in_ref, terms_ref):
    gn_ref[...] = rc_ref[:, :TT].astype(F32)
    for j in range(TILES):
        gn_ref[warp[j]] += rc_ref[j, TT : 2 * TT].astype(F32)
    total = jnp.sum(rc_ref[:, 2 * TT :].astype(F32), axis=0)
    terms_ref[...] = total[0:3] + total[3:6]
    prod = gn_ref[...] * sp_ref[...].astype(F32)
    prod = prod.reshape(TOK, HERE * HD)
    prod = sum(prod[:, h * HD : (h + 1) * HD] for h in range(HERE))
    in_ref[...] = row_sums(prod)[0:1]


def spatial_backward(
    q_ref, k_ref, v_ref, p_ref, sp_ref, gn_ref, s1_ref, s2_ref, i1_ref, i2_ref,
    dq_ref, dk_ref, dv_ref, inv_s, shift, gb, ts,
):
    h = pl.program_id(0)

    @pl.when(h == 0)
    def _():
        inv = lax.rsqrt((s1_ref[...] + s2_ref[...]) / WIDTH + EPS)
        inv_s[...] = as_column(inv)
        shift[...] = as_column(inv * inv * inv * ((i1_ref[...] + i2_ref[...]) / WIDTH))

    k = k_ref[:, lanes(h)]
    v = v_ref[:, lanes(h)]
    for i in range(BLOCKS):
        rows = slice(i * RB, (i + 1) * RB)
        spatial = sp_ref[rows, lanes(h)].astype(F32)
        grad = inv_s[rows, :] * gn_ref[rows, lanes(h)] - spatial * shift[rows, :]
        g = grad.astype(BF16)
        gb[rows, :] = g
        inner = jnp.sum(g.astype(F32) * spatial, axis=-1, keepdims=True)
        t = p_ref[h, rows, :] * (dot_nt(g, v) - inner).astype(BF16)
        ts[rows, :] = t
        dq_ref[rows, :] = (dot_nn(t, k) * SCALE).astype(BF16)
    dk_ref[...] = (dot_nn(q_ref[:, lanes(h)].T, ts[...]) * SCALE).T.astype(BF16)
    dv_ref[...] = dot_nn(gb[...].T, p_ref[h]).T.astype(BF16)


def columns(rows=TOK):
    return pl.BlockSpec((rows, HD), lambda h, *_: (0, h))


def call(kernel, grid, in_specs, out_specs, out_shape, scratch, us, prefetch=0, limit=24):
    return pl.pallas_call(
        kernel,
        grid_spec=pltpu.PrefetchScalarGridSpec(
            num_scalar_prefetch=prefetch,
            grid=grid,
            in_specs=in_specs,
            out_specs=out_specs,
            scratch_shapes=scratch,
        ),
        out_shape=out_shape,
        cost_estimate=pl.CostEstimate(
            flops=int(us * 1e6), bytes_accessed=int(us * 3.0e6), transcendentals=0
        ),
        compiler_params=pltpu.CompilerParams(vmem_limit_bytes=limit * 1024 * 1024),
    )


def swapped(x, axis, flip):
    size = lax.axis_size(axis)
    return lax.ppermute(x, axis, [(i, i ^ flip) for i in range(size)])


def half_sums(x, axis):
    other = swapped(x, axis, 1)
    x = x + other
    return x, swapped(x, axis, 2)


def exchanged(x):
    return lax.all_to_all(x, "frame", 0, 0, tiled=True)


def body(query_spatial, key_spatial, value_spatial, gains, warp_lists, cotangent):
    width = HERE * HD
    q = query_spatial.reshape(TOK, width)
    k = key_spatial.reshape(TOK, width)
    v = value_spatial.reshape(TOK, width)
    g = cotangent.reshape(TOK, width)
    warp = warp_lists[0, 0]
    sds = jax.ShapeDtypeStruct
    tall = pltpu.VMEM((TOK, HD), F32)
    thin = pltpu.VMEM((TOK, HD), BF16)
    big = pltpu.VMEM((TOK, TOK), BF16)
    held = pl.BlockSpec(memory_space=pltpu.VMEM)
    away = pl.BlockSpec(memory_space=pltpu.HBM)
    line = sds((1, TOK), F32)
    flat = sds((TOK, width), BF16)
    three = sds((3, width), F32)
    heads = (HERE,)

    spatial, probs, squares = call(
        spatial_forward,
        heads,
        [away] * 3,
        [held] * 3,
        [flat, sds((HERE, TOK, TOK), BF16), line],
        [big, big, big, tall, pltpu.SemaphoreType.DMA((3, HERE))],
        7,
    )(*(pltpu.with_memory_space_constraint(x, pltpu.HBM) for x in (q, k, v)))
    ss_one, ss_two = half_sums(squares, "mp")
    spatial_tiles = spatial.reshape(TILES, TT, width)
    send = call(
        pack_normed,
        (),
        [held] * 3,
        held,
        sds((TILES, 2 * TT, width), BF16),
        [pltpu.VMEM((TILES, TT, width), BF16)],
        1,
        prefetch=1,
    )(warp, spatial_tiles, ss_one, ss_two)
    got = exchanged(send)

    out, back = call(
        temporal,
        heads,
        [held] * 3,
        [columns(), held],
        [flat, sds((TILES, 2 * TT + 8, width), BF16)],
        [thin, thin, thin, big, big, tall, pltpu.VMEM((8, HD), F32)],
        16,
    )(got, g, gains)
    came = exchanged(back)

    grad_normed, inner, terms = call(
        gather_back,
        (),
        [held] * 2,
        [held] * 3,
        [sds((TILES, TT, width), F32), line, three],
        [],
        2,
        prefetch=1,
    )(warp, came, spatial_tiles)
    in_one, in_two = half_sums(inner, "mp")
    t_one, t_two = half_sums(terms, "clip")

    dq, dk, dv = call(
        spatial_backward,
        heads,
        [held] * 10,
        [columns()] * 3,
        [flat] * 3,
        [tall, tall, thin, big],
        9,
    )(
        q, k, v, probs, spatial, grad_normed.reshape(TOK, width),
        ss_one, ss_two, in_one, in_two,
    )
    return (
        out.reshape(cotangent.shape),
        dq.reshape(query_spatial.shape),
        dk.reshape(query_spatial.shape),
        dv.reshape(query_spatial.shape),
        t_one + t_two,
    )


def solution(mesh):
    frames = P("clip", "frame", None, None, "mp")
    tiles = P("clip", None, "frame", None, "mp")
    return jax.shard_map(
        body,
        mesh=mesh,
        in_specs=(frames, frames, frames, P(None, "mp"), P("clip", "frame", None), tiles),
        out_specs=(tiles, frames, frames, frames, P(None, "mp")),
        check_vma=False,
    )
```

```python
import math

import jax
import jax.numpy as jnp
from jax import lax
from jax.experimental import pallas as pl
from jax.experimental.pallas import tpu as pltpu
from jax.sharding import PartitionSpec as P


HEADS = 20
HD = 128
TILES = 16
TT = 40
TOK = TILES * TT
WIDTH = HEADS * HD
HERE = 5
EPS = 1e-06
SCALE = 1.0 / math.sqrt(HD)
LOG2E = math.log2(math.e)
RB = 320
SUB = 160
BLOCKS = TOK // RB
F32 = jnp.float32
BF16 = jnp.bfloat16


def dot_nt(a, b):
    return lax.dot_general(a, b, (((1,), (1,)), ((), ())), preferred_element_type=F32)


def dot_nn(a, b):
    return lax.dot_general(a, b, (((1,), (0,)), ((), ())), preferred_element_type=F32)


def row_sums(x):
    ones = jnp.ones((8, x.shape[1]), F32)
    return lax.dot_general(
        ones, x, (((1,), (1,)), ((), ())), preferred_element_type=F32, precision=lax.Precision.HIGHEST
    )


def column_sum(x):
    x = jnp.sum(x.reshape(10, 64, HD), axis=0)
    return jnp.sum(x, axis=0, keepdims=True)


def as_column(row):
    return jnp.broadcast_to(row, (128, row.shape[1])).T


def softmax_rows(s):
    top = jnp.max(s, axis=-1, keepdims=True)
    e = jnp.exp2((s - top) * (SCALE * LOG2E))
    return (e * (1.0 / jnp.sum(e, axis=-1, keepdims=True))).astype(BF16)


def lanes(h):
    return pl.ds(pl.multiple_of(h * HD, HD), HD)


def spatial_forward(q_hbm, k_hbm, v_hbm, o_ref, p_ref, ss_ref, q_ref, k_ref, v_ref, acc, sems):
    h = pl.program_id(0)

    def copies(n):
        return [
            pltpu.make_async_copy(a.at[:, lanes(n)], b.at[:, lanes(n)], sems.at[i, n])
            for i, (a, b) in enumerate(((k_hbm, k_ref), (q_hbm, q_ref), (v_hbm, v_ref)))
        ]

    @pl.when(h == 0)
    def _():
        for n in range(HERE):
            for copy in copies(n):
                copy.start()
        acc[...] = jnp.zeros_like(acc)

    for copy in copies(h):
        copy.wait()

    k = k_ref[:, lanes(h)]
    vw = jnp.concatenate([v_ref[:, lanes(h)], jnp.ones((TOK, HD), BF16)], axis=1)
    for i in range(BLOCKS):
        rows = slice(i * RB, (i + 1) * RB)
        p = softmax_rows(dot_nt(q_ref[rows, lanes(h)], k))
        p_ref[h, rows, :] = p
        o = dot_nn(p, vw)[:, :HD].astype(BF16)
        o_ref[rows, lanes(h)] = o
        of = o.astype(F32)
        acc[rows, :] += of * of

    @pl.when(h == HERE - 1)
    def _():
        ss_ref[...] = row_sums(acc[...])[0:1]


def pack_normed(warp, sp_ref, one_ref, two_ref, send_ref, n_ref):
    inv = lax.rsqrt((one_ref[...] + two_ref[...]) / WIDTH + EPS)
    inv = as_column(inv)
    for j in range(TILES):
        col = inv[j * TT : (j + 1) * TT]
        normed = (sp_ref[j].astype(F32) * jnp.concatenate([col] * HERE, axis=1)).astype(BF16)
        n_ref[j] = normed
        send_ref[j, :TT] = normed
    for j in range(TILES):
        send_ref[j, TT:] = n_ref[warp[j]]


def temporal(rc_ref, g_ref, gain_ref, out_ref, send_ref, qs, ks, vs, ps, ts, ds, terms):
    h = pl.program_id(0)

    @pl.when(h == 0)
    def _():
        ps[...] = jnp.zeros_like(ps)
        ts[...] = jnp.zeros_like(ts)

    gq, gk, gv = gain_ref[0:1, lanes(h)], gain_ref[1:2, lanes(h)], gain_ref[2:3, lanes(h)]
    normed = rc_ref[:, :TT, lanes(h)].astype(F32).reshape(TOK, HD)
    warped = rc_ref[:, TT:, lanes(h)].astype(F32).reshape(TOK, HD)
    qs[...] = (normed * gq).astype(BF16)
    ks[...] = (warped * gk).astype(BF16)
    vs[...] = (warped * gv).astype(BF16)
    s = dot_nt(qs[...], ks[...])
    spans = []
    for i in range(0, TOK, SUB):
        rows = slice(i, i + SUB)
        last = ((i + SUB - 1) // TT + 1) * TT
        keys = min(-(-last // HD) * HD, TOK)
        clear = (i // TT + 1) * TT // HD * HD
        spans.append((rows, keys))
        row = lax.broadcasted_iota(jnp.int32, (SUB, 1), 0).astype(F32) + (i + 0.5)
        limit = (jnp.floor(row * (1.0 / TT)) + 1.0) * TT
        if clear < keys:
            col = lax.broadcasted_iota(jnp.int32, (SUB, keys - clear), 1).astype(F32) + clear
            part = jnp.where(col < limit, s[rows, clear:keys], -1e30)
            part = jnp.concatenate([s[rows, :clear], part], axis=1) if clear else part
        else:
            part = s[rows, :keys]
        ps[rows, :keys] = softmax_rows(part)
    o = dot_nn(ps[...], vs[...])
    out_ref[...] = o.astype(BF16)
    g = g_ref[:, lanes(h)]
    inner = jnp.sum(g.astype(F32) * o, axis=-1, keepdims=True)
    dp = dot_nt(g, vs[...])
    for rows, keys in spans:
        ts[rows, :keys] = ps[rows, :keys] * (dp[rows, :keys] - inner[rows]).astype(BF16)
    ds[...] = dot_nn(ts[...], ks[...]) * SCALE

    def by_keys(lt, right):
        parts = [
            dot_nn(lt, right[:, : 2 * HD]),
            dot_nn(lt[:, HD:], right[HD:, 2 * HD : 4 * HD]),
            dot_nn(lt[:, 3 * HD :], right[3 * HD :, 4 * HD :]),
        ]
        return jnp.concatenate([x.T for x in parts], axis=0)

    dk = by_keys(qs[...].T, ts) * SCALE
    dv = by_keys(g_ref[:, lanes(h)].T, ps)
    dq = ds[...]
    normed = rc_ref[:, :TT, lanes(h)].astype(F32).reshape(TOK, HD)
    warped = rc_ref[:, TT:, lanes(h)].astype(F32).reshape(TOK, HD)
    start = pl.multiple_of(h * 2 * TT, 16)
    send_ref[:, pl.ds(start, TT), :] = (dq * gq).reshape(TILES, TT, HD).astype(BF16)
    start = pl.multiple_of(start + TT, 8)
    send_ref[:, pl.ds(start, TT), :] = (dk * gk + dv * gv).reshape(TILES, TT, HD).astype(BF16)
    terms[0:1, lanes(h)] = column_sum(dq * normed)
    terms[1:2, lanes(h)] = column_sum(dk * warped)
    terms[2:3, lanes(h)] = column_sum(dv * warped)

    @pl.when(h == HERE - 1)
    def _():
        blocks = [terms[n // HERE : n // HERE + 1, n % HERE * HD : n % HERE * HD + HD] for n in range(3 * HERE)]
        stack = jnp.concatenate(blocks + [blocks[0]], axis=0)
        send_ref[:, HERE * 2 * TT :, :] = jnp.broadcast_to(stack[None], (TILES, 16, HD)).astype(BF16)


def gather_back(warp, rc_ref, sp_ref, gn_ref, in_ref, terms_ref):
    total = jnp.sum(rc_ref[:, HERE * 2 * TT :].astype(F32), axis=0)
    for n in range(3 * HERE):
        at = n % HERE * HD
        terms_ref[n // HERE : n // HERE + 1, at : at + HD] = total[n : n + 1]
    inner = jnp.zeros((TOK, HD), F32)
    for h in range(HERE):
        cols = slice(h * HD, (h + 1) * HD)
        first = h * 2 * TT
        gn_ref[:, :, cols] = rc_ref[:, first : first + TT].astype(F32)
        for j in range(TILES):
            gn_ref[warp[j], :, cols] += rc_ref[j, first + TT : first + 2 * TT].astype(F32)
        prod = gn_ref[:, :, cols] * sp_ref[:, :, cols].astype(F32)
        inner += prod.reshape(TOK, HD)
    in_ref[...] = row_sums(inner)[0:1]


def spatial_backward(
    q_ref, k_ref, v_ref, p_ref, sp_ref, gn_ref, s1_ref, s2_ref, i1_ref, i2_ref,
    dq_ref, dk_ref, dv_ref, inv_s, shift, gb, ts,
):
    h = pl.program_id(0)

    @pl.when(h == 0)
    def _():
        inv = lax.rsqrt((s1_ref[...] + s2_ref[...]) / WIDTH + EPS)
        inv_s[...] = as_column(inv)
        shift[...] = as_column(inv * inv * inv * ((i1_ref[...] + i2_ref[...]) / WIDTH))

    k = k_ref[:, lanes(h)]
    v = v_ref[:, lanes(h)]
    for i in range(BLOCKS):
        rows = slice(i * RB, (i + 1) * RB)
        spatial = sp_ref[rows, lanes(h)].astype(F32)
        grad = inv_s[rows, :] * gn_ref[rows, lanes(h)] - spatial * shift[rows, :]
        g = grad.astype(BF16)
        gb[rows, :] = g
        inner = jnp.sum(g.astype(F32) * spatial, axis=-1, keepdims=True)
        t = p_ref[h, rows, :] * (dot_nt(g, v) - inner).astype(BF16)
        ts[rows, :] = t
        dq_ref[rows, :] = (dot_nn(t, k) * SCALE).astype(BF16)
    dk_ref[...] = (dot_nn(q_ref[:, lanes(h)].T, ts[...]) * SCALE).T.astype(BF16)
    dv_ref[...] = dot_nn(gb[...].T, p_ref[h]).T.astype(BF16)


def columns(rows=TOK):
    return pl.BlockSpec((rows, HD), lambda h, *_: (0, h))


def call(kernel, grid, in_specs, out_specs, out_shape, scratch, us, prefetch=0, limit=24):
    return pl.pallas_call(
        kernel,
        grid_spec=pltpu.PrefetchScalarGridSpec(
            num_scalar_prefetch=prefetch,
            grid=grid,
            in_specs=in_specs,
            out_specs=out_specs,
            scratch_shapes=scratch,
        ),
        out_shape=out_shape,
        cost_estimate=pl.CostEstimate(
            flops=int(us * 1e6), bytes_accessed=int(us * 3.0e6), transcendentals=0
        ),
        compiler_params=pltpu.CompilerParams(vmem_limit_bytes=limit * 1024 * 1024),
    )


def swapped(x, axis, flip):
    size = lax.axis_size(axis)
    return lax.ppermute(x, axis, [(i, i ^ flip) for i in range(size)])


def half_sums(x, axis):
    other = swapped(x, axis, 1)
    x = x + other
    return x, swapped(x, axis, 2)


def exchanged(x):
    return lax.all_to_all(x, "frame", 0, 0, tiled=True)


def body(query_spatial, key_spatial, value_spatial, gains, warp_lists, cotangent):
    width = HERE * HD
    q = query_spatial.reshape(TOK, width)
    k = key_spatial.reshape(TOK, width)
    v = value_spatial.reshape(TOK, width)
    g = cotangent.reshape(TOK, width)
    warp = warp_lists[0, 0]
    sds = jax.ShapeDtypeStruct
    tall = pltpu.VMEM((TOK, HD), F32)
    thin = pltpu.VMEM((TOK, HD), BF16)
    big = pltpu.VMEM((TOK, TOK), BF16)
    held = pl.BlockSpec(memory_space=pltpu.VMEM)
    away = pl.BlockSpec(memory_space=pltpu.HBM)
    line = sds((1, TOK), F32)
    flat = sds((TOK, width), BF16)
    three = sds((3, width), F32)
    heads = (HERE,)

    spatial, probs, squares = call(
        spatial_forward,
        heads,
        [away] * 3,
        [held] * 3,
        [flat, sds((HERE, TOK, TOK), BF16), line],
        [big, big, big, tall, pltpu.SemaphoreType.DMA((3, HERE))],
        7,
    )(*(pltpu.with_memory_space_constraint(x, pltpu.HBM) for x in (q, k, v)))
    ss_one, ss_two = half_sums(squares, "mp")
    spatial_tiles = spatial.reshape(TILES, TT, width)
    send = call(
        pack_normed,
        (),
        [held] * 3,
        held,
        sds((TILES, 2 * TT, width), BF16),
        [pltpu.VMEM((TILES, TT, width), BF16)],
        1,
        prefetch=1,
    )(warp, spatial_tiles, ss_one, ss_two)
    got = exchanged(send)

    out, back = call(
        temporal,
        heads,
        [held] * 3,
        [columns(), held],
        [flat, sds((TILES, HERE * 2 * TT + 16, HD), BF16)],
        [thin, thin, thin, big, big, tall, pltpu.VMEM((8, width), F32)],
        16,
    )(got, g, gains)
    came = exchanged(back)

    grad_normed, inner, terms = call(
        gather_back,
        (),
        [held] * 2,
        [held] * 3,
        [sds((TILES, TT, width), F32), line, three],
        [],
        2,
        prefetch=1,
    )(warp, came, spatial_tiles)
    in_one, in_two = half_sums(inner, "mp")
    t_one, t_two = half_sums(terms, "clip")

    dq, dk, dv = call(
        spatial_backward,
        heads,
        [held] * 10,
        [columns()] * 3,
        [flat] * 3,
        [tall, tall, thin, big],
        9,
    )(
        q, k, v, probs, spatial, grad_normed.reshape(TOK, width),
        ss_one, ss_two, in_one, in_two,
    )
    return (
        out.reshape(cotangent.shape),
        dq.reshape(query_spatial.shape),
        dk.reshape(query_spatial.shape),
        dv.reshape(query_spatial.shape),
        t_one + t_two,
    )


def solution(mesh):
    frames = P("clip", "frame", None, None, "mp")
    tiles = P("clip", None, "frame", None, "mp")
    return jax.shard_map(
        body,
        mesh=mesh,
        in_specs=(frames, frames, frames, P(None, "mp"), P("clip", "frame", None), tiles),
        out_specs=(tiles, frames, frames, frames, P(None, "mp")),
        check_vma=False,
    )
```

```python
import math

import jax
import jax.numpy as jnp
from jax import lax
from jax.experimental import pallas as pl
from jax.experimental.pallas import tpu as pltpu
from jax.sharding import PartitionSpec as P


HEADS = 20
HD = 128
TILES = 16
TT = 40
TOK = TILES * TT
WIDTH = HEADS * HD
HERE = 5
EPS = 1e-06
SCALE = 1.0 / math.sqrt(HD)
LOG2E = math.log2(math.e)
RB = 320
SUB = 160
BLOCKS = TOK // RB
F32 = jnp.float32
BF16 = jnp.bfloat16


def dot_nt(a, b):
    return lax.dot_general(a, b, (((1,), (1,)), ((), ())), preferred_element_type=F32)


def dot_nn(a, b):
    return lax.dot_general(a, b, (((1,), (0,)), ((), ())), preferred_element_type=F32)


def row_sums(x):
    ones = jnp.ones((8, x.shape[1]), F32)
    return lax.dot_general(
        ones, x, (((1,), (1,)), ((), ())), preferred_element_type=F32, precision=lax.Precision.HIGHEST
    )


def column_sum(x):
    x = jnp.sum(x.reshape(10, 64, HD), axis=0)
    return jnp.sum(x, axis=0, keepdims=True)


def as_column(row):
    return jnp.broadcast_to(row, (128, row.shape[1])).T


def softmax_rows(s):
    top = jnp.max(s, axis=-1, keepdims=True)
    e = jnp.exp2((s - top) * (SCALE * LOG2E))
    return (e * (1.0 / jnp.sum(e, axis=-1, keepdims=True))).astype(BF16)


def lanes(h):
    return pl.ds(pl.multiple_of(h * HD, HD), HD)


def spatial_forward(q_hbm, k_hbm, v_hbm, o_ref, p_ref, ss_ref, q_ref, k_ref, v_ref, acc, sems):
    h = pl.program_id(0)

    def copies(n):
        return [
            pltpu.make_async_copy(a.at[:, lanes(n)], b.at[:, lanes(n)], sems.at[i, n])
            for i, (a, b) in enumerate(((k_hbm, k_ref), (q_hbm, q_ref), (v_hbm, v_ref)))
        ]

    @pl.when(h == 0)
    def _():
        for n in range(HERE):
            for copy in copies(n):
                copy.start()
        acc[...] = jnp.zeros_like(acc)

    for copy in copies(h):
        copy.wait()

    k = k_ref[:, lanes(h)]
    vw = jnp.concatenate([v_ref[:, lanes(h)], jnp.ones((TOK, HD), BF16)], axis=1)
    for i in range(BLOCKS):
        rows = slice(i * RB, (i + 1) * RB)
        p = softmax_rows(dot_nt(q_ref[rows, lanes(h)], k))
        p_ref[h, rows, :] = p
        o = dot_nn(p, vw)[:, :HD].astype(BF16)
        o_ref[rows, lanes(h)] = o
        of = o.astype(F32)
        acc[rows, :] += of * of

    @pl.when(h == HERE - 1)
    def _():
        ss_ref[...] = row_sums(acc[...])[0:1]


def pack_normed(warp, sp_ref, one_ref, two_ref, send_ref, n_ref):
    inv = lax.rsqrt((one_ref[...] + two_ref[...]) / WIDTH + EPS)
    inv = as_column(inv)
    for j in range(TILES):
        col = inv[j * TT : (j + 1) * TT]
        normed = (sp_ref[j].astype(F32) * jnp.concatenate([col] * HERE, axis=1)).astype(BF16)
        n_ref[j] = normed
        send_ref[j, :TT] = normed
    for j in range(TILES):
        send_ref[j, TT:] = n_ref[warp[j]]


def temporal(rc_ref, g_ref, gain_ref, out_ref, send_ref, qs, ks, vs, ps, ts, ds, terms):
    h = pl.program_id(0)

    @pl.when(h == 0)
    def _():
        ps[...] = jnp.zeros_like(ps)
        ts[...] = jnp.zeros_like(ts)

    gq, gk, gv = gain_ref[0:1, lanes(h)], gain_ref[1:2, lanes(h)], gain_ref[2:3, lanes(h)]
    normed = rc_ref[:, :TT, lanes(h)].astype(F32).reshape(TOK, HD)
    warped = rc_ref[:, TT:, lanes(h)].astype(F32).reshape(TOK, HD)
    qs[...] = (normed * gq).astype(BF16)
    ks[...] = (warped * gk).astype(BF16)
    vs[...] = (warped * gv).astype(BF16)
    s = dot_nt(qs[...], ks[...])
    spans = []
    for i in range(0, TOK, SUB):
        rows = slice(i, i + SUB)
        last = ((i + SUB - 1) // TT + 1) * TT
        keys = min(-(-last // HD) * HD, TOK)
        clear = (i // TT + 1) * TT // HD * HD
        spans.append((rows, keys))
        row = lax.broadcasted_iota(jnp.int32, (SUB, 1), 0).astype(F32) + (i + 0.5)
        limit = (jnp.floor(row * (1.0 / TT)) + 1.0) * TT
        if clear < keys:
            col = lax.broadcasted_iota(jnp.int32, (SUB, keys - clear), 1).astype(F32) + clear
            part = jnp.where(col < limit, s[rows, clear:keys], -1e30)
            part = jnp.concatenate([s[rows, :clear], part], axis=1) if clear else part
        else:
            part = s[rows, :keys]
        ps[rows, :keys] = softmax_rows(part)
    o = dot_nn(ps[...], vs[...])
    out_ref[...] = o.astype(BF16)
    g = g_ref[:, lanes(h)]
    inner = jnp.sum(g.astype(F32) * o, axis=-1, keepdims=True)
    dp = dot_nt(g, vs[...])
    for rows, keys in spans:
        ts[rows, :keys] = ps[rows, :keys] * (dp[rows, :keys] - inner[rows]).astype(BF16)
    ds[...] = dot_nn(ts[...], ks[...]) * SCALE

    def by_keys(lt, right):
        parts = [
            dot_nn(lt, right[:, : 2 * HD]),
            dot_nn(lt[:, HD:], right[HD:, 2 * HD : 4 * HD]),
            dot_nn(lt[:, 3 * HD :], right[3 * HD :, 4 * HD :]),
        ]
        return jnp.concatenate([x.T for x in parts], axis=0)

    dk = by_keys(qs[...].T, ts) * SCALE
    dv = by_keys(g_ref[:, lanes(h)].T, ps)
    dq = ds[...]
    normed = rc_ref[:, :TT, lanes(h)].astype(F32).reshape(TOK, HD)
    warped = rc_ref[:, TT:, lanes(h)].astype(F32).reshape(TOK, HD)
    direct = (dq * gq).reshape(TILES, TT, HD).astype(BF16)
    moved = (dk * gk + dv * gv).reshape(TILES, TT, HD).astype(BF16)
    for n in range(HERE):

        @pl.when(h == n)
        def _(n=n):
            send_ref[:, 2 * n * TT : (2 * n + 1) * TT, :] = direct
            send_ref[:, (2 * n + 1) * TT : (2 * n + 2) * TT, :] = moved

    terms[0:1, lanes(h)] = column_sum(dq * normed)
    terms[1:2, lanes(h)] = column_sum(dk * warped)
    terms[2:3, lanes(h)] = column_sum(dv * warped)

    @pl.when(h == HERE - 1)
    def _():
        blocks = [terms[n // HERE : n // HERE + 1, n % HERE * HD : n % HERE * HD + HD] for n in range(3 * HERE)]
        stack = jnp.concatenate(blocks + [blocks[0]], axis=0)
        send_ref[:, HERE * 2 * TT :, :] = jnp.broadcast_to(stack[None], (TILES, 16, HD)).astype(BF16)


def gather_back(warp, rc_ref, sp_ref, gn_ref, in_ref, terms_ref):
    total = jnp.sum(rc_ref[:, HERE * 2 * TT :].astype(F32), axis=0)
    for n in range(3 * HERE):
        at = n % HERE * HD
        terms_ref[n // HERE : n // HERE + 1, at : at + HD] = total[n : n + 1]
    inner = jnp.zeros((TOK, HD), F32)
    for h in range(HERE):
        cols = slice(h * HD, (h + 1) * HD)
        first = h * 2 * TT
        gn_ref[:, :, cols] = rc_ref[:, first : first + TT].astype(F32)
        for j in range(TILES):
            gn_ref[warp[j], :, cols] += rc_ref[j, first + TT : first + 2 * TT].astype(F32)
        prod = gn_ref[:, :, cols] * sp_ref[:, :, cols].astype(F32)
        inner += prod.reshape(TOK, HD)
    in_ref[...] = row_sums(inner)[0:1]


def spatial_backward(
    q_ref, k_ref, v_ref, p_ref, sp_ref, gn_ref, s1_ref, s2_ref, i1_ref, i2_ref,
    dq_ref, dk_ref, dv_ref, inv_s, shift, gb, ts,
):
    h = pl.program_id(0)

    @pl.when(h == 0)
    def _():
        inv = lax.rsqrt((s1_ref[...] + s2_ref[...]) / WIDTH + EPS)
        inv_s[...] = as_column(inv)
        shift[...] = as_column(inv * inv * inv * ((i1_ref[...] + i2_ref[...]) / WIDTH))

    k = k_ref[:, lanes(h)]
    v = v_ref[:, lanes(h)]
    for i in range(BLOCKS):
        rows = slice(i * RB, (i + 1) * RB)
        spatial = sp_ref[rows, lanes(h)].astype(F32)
        grad = inv_s[rows, :] * gn_ref[rows, lanes(h)] - spatial * shift[rows, :]
        g = grad.astype(BF16)
        gb[rows, :] = g
        inner = jnp.sum(g.astype(F32) * spatial, axis=-1, keepdims=True)
        t = p_ref[h, rows, :] * (dot_nt(g, v) - inner).astype(BF16)
        ts[rows, :] = t
        dq_ref[rows, :] = (dot_nn(t, k) * SCALE).astype(BF16)
    dk_ref[...] = (dot_nn(q_ref[:, lanes(h)].T, ts[...]) * SCALE).T.astype(BF16)
    dv_ref[...] = dot_nn(gb[...].T, p_ref[h]).T.astype(BF16)


def columns(rows=TOK):
    return pl.BlockSpec((rows, HD), lambda h, *_: (0, h))


def call(kernel, grid, in_specs, out_specs, out_shape, scratch, us, prefetch=0, limit=24):
    return pl.pallas_call(
        kernel,
        grid_spec=pltpu.PrefetchScalarGridSpec(
            num_scalar_prefetch=prefetch,
            grid=grid,
            in_specs=in_specs,
            out_specs=out_specs,
            scratch_shapes=scratch,
        ),
        out_shape=out_shape,
        cost_estimate=pl.CostEstimate(
            flops=int(us * 1e6), bytes_accessed=int(us * 3.0e6), transcendentals=0
        ),
        compiler_params=pltpu.CompilerParams(vmem_limit_bytes=limit * 1024 * 1024),
    )


def swapped(x, axis, flip):
    size = lax.axis_size(axis)
    return lax.ppermute(x, axis, [(i, i ^ flip) for i in range(size)])


def half_sums(x, axis):
    other = swapped(x, axis, 1)
    x = x + other
    return x, swapped(x, axis, 2)


def exchanged(x):
    return lax.all_to_all(x, "frame", 0, 0, tiled=True)


def body(query_spatial, key_spatial, value_spatial, gains, warp_lists, cotangent):
    width = HERE * HD
    q = query_spatial.reshape(TOK, width)
    k = key_spatial.reshape(TOK, width)
    v = value_spatial.reshape(TOK, width)
    g = cotangent.reshape(TOK, width)
    warp = warp_lists[0, 0]
    sds = jax.ShapeDtypeStruct
    tall = pltpu.VMEM((TOK, HD), F32)
    thin = pltpu.VMEM((TOK, HD), BF16)
    big = pltpu.VMEM((TOK, TOK), BF16)
    held = pl.BlockSpec(memory_space=pltpu.VMEM)
    away = pl.BlockSpec(memory_space=pltpu.HBM)
    line = sds((1, TOK), F32)
    flat = sds((TOK, width), BF16)
    three = sds((3, width), F32)
    heads = (HERE,)

    spatial, probs, squares = call(
        spatial_forward,
        heads,
        [away] * 3,
        [held] * 3,
        [flat, sds((HERE, TOK, TOK), BF16), line],
        [big, big, big, tall, pltpu.SemaphoreType.DMA((3, HERE))],
        7,
    )(*(pltpu.with_memory_space_constraint(x, pltpu.HBM) for x in (q, k, v)))
    ss_one, ss_two = half_sums(squares, "mp")
    spatial_tiles = spatial.reshape(TILES, TT, width)
    send = call(
        pack_normed,
        (),
        [held] * 3,
        held,
        sds((TILES, 2 * TT, width), BF16),
        [pltpu.VMEM((TILES, TT, width), BF16)],
        1,
        prefetch=1,
    )(warp, spatial_tiles, ss_one, ss_two)
    got = exchanged(send)

    out, back = call(
        temporal,
        heads,
        [held] * 3,
        [columns(), held],
        [flat, sds((TILES, HERE * 2 * TT + 16, HD), BF16)],
        [thin, thin, thin, big, big, tall, pltpu.VMEM((8, width), F32)],
        16,
    )(got, g, gains)
    came = exchanged(back)

    grad_normed, inner, terms = call(
        gather_back,
        (),
        [held] * 2,
        [held] * 3,
        [sds((TILES, TT, width), F32), line, three],
        [],
        2,
        prefetch=1,
    )(warp, came, spatial_tiles)
    in_one, in_two = half_sums(inner, "mp")
    t_one, t_two = half_sums(terms, "clip")

    dq, dk, dv = call(
        spatial_backward,
        heads,
        [held] * 10,
        [columns()] * 3,
        [flat] * 3,
        [tall, tall, thin, big],
        9,
    )(
        q, k, v, probs, spatial, grad_normed.reshape(TOK, width),
        ss_one, ss_two, in_one, in_two,
    )
    return (
        out.reshape(cotangent.shape),
        dq.reshape(query_spatial.shape),
        dk.reshape(query_spatial.shape),
        dv.reshape(query_spatial.shape),
        t_one + t_two,
    )


def solution(mesh):
    frames = P("clip", "frame", None, None, "mp")
    tiles = P("clip", None, "frame", None, "mp")
    return jax.shard_map(
        body,
        mesh=mesh,
        in_specs=(frames, frames, frames, P(None, "mp"), P("clip", "frame", None), tiles),
        out_specs=(tiles, frames, frames, frames, P(None, "mp")),
        check_vma=False,
    )
```
